256 devices in a mesh: energy: 128 (over z, y, x), mom: 2 (over core).
Axes of the slice: x: 4, y: 4, z: 8, core: 2. Of those that a mesh axis runs over, the one named last changes fastest.
Arguments:
- lesser: bfloat16 [2, 2, 512, 65536], P('mom', None, 'energy'), may hold values from -6 to 6
- greater: bfloat16 [2, 2, 512, 65536], P('mom', None, 'energy'), may hold values from -6 to 6
- coulomb: bfloat16 [2, 4, 128, 128], P('mom'), may hold values from -0.375 to 0.375
- tile_block: int32 [4], replicated, may hold values from 0 to 3, each once
- shift_table: int32 [2, 2], replicated, may hold values from 0 to 1, each once within a row
Outputs:
- polarization: bfloat16 [2, 2, 512, 65536], P('mom', None, 'energy')
- screened: float32 [2, 2, 128, 65536], P('mom', None, 'energy')
The draws below stay inside these ranges and needn't reach their ends.
Inputs may be any that keep to these rules, and one draw needn't show every extreme that they name: `tile_block`: each of the 4 tiles holds a different block of the pattern. `shift_table`: each row names every momentum once.
All inputs are finite; a program needn't handle non-finite values.
Results may differ from the reference program's by a relative error of at most 0.0013.
Values may be sent and summed in bfloat16 or wider, within the bound.
A program may use at most 128 MiB of HBM per device.

```python
import math
import jax
import jax.numpy as jnp
from jax import lax

E = 512
NK = 2
BS = 128
NBW = 2
NT = 4
NNZ = 65536


def levels(key, shape, split, low, largest):
    loudness, own = 1.0, jax.random.fold_in(key, 6)
    for axis_at, shards_of in split:
        heights = jnp.exp(jax.random.uniform(jax.random.fold_in(own, axis_at), (shards_of,), jnp.float32, low / len(split), largest / len(split)))
        loudness = loudness * jnp.repeat(heights, shape[axis_at] // shards_of).reshape([-1 if axis == axis_at else 1 for axis in range(len(shape))])
    return loudness


def normal_values(own_key, shape, scale, bound, pieces=(), held_as=jnp.bfloat16):
    factor_of = levels(own_key, shape, pieces, -0.22, 0.18) if pieces else 1.0
    array = jax.random.normal(own_key, shape, jnp.float32) * scale * factor_of
    return jnp.minimum(jnp.maximum(array, -bound), bound).astype(held_as)


def setup_inputs(seed: int = 0) -> dict:
    arg_keys = jax.random.split(jax.random.key(seed), 6)
    return {
        "lesser": normal_values(arg_keys[0], (NK, 2, E, NNZ), 1.0, 6.0, ((0, 2), (2, 128))),
        "greater": normal_values(arg_keys[1], (NK, 2, E, NNZ), 1.0, 6.0, ((0, 2), (2, 128))),
        "coulomb": normal_values(arg_keys[2], (NK, NT, BS, BS), (2 * BS) ** -0.5, 0.375, ((0, 2),)),
        "tile_block": jax.random.permutation(arg_keys[3], NT).astype(jnp.int32),
        "shift_table": jax.vmap(lambda own: jax.random.permutation(own, NK))(jax.random.split(arg_keys[4], NK)).reshape((NK, NK)).astype(jnp.int32),
    }


def pattern_blocks(count):
    return [(r, c) for r in range(count) for c in range(max(0, r - 1), min(count, r + 2))]

def polar_columns(lesser, greater, shift_table, start, width):
    left = lax.dynamic_slice_in_dim(lesser, start, width, 3).astype(jnp.float32)
    right = lax.dynamic_slice_in_dim(greater, start, width, 3).astype(jnp.float32)
    left_spec = jnp.fft.fft(lax.complex(left[:, 0], left[:, 1]), n=2 * E, axis=1)
    right_spec = jnp.fft.fft(lax.complex(right[:, 0], right[:, 1]), n=2 * E, axis=1)
    paired = jnp.take(right_spec, shift_table, axis=0)
    total = lax.optimization_barrier(jnp.sum(left_spec[None] * jnp.conj(paired), axis=1))
    corr = jnp.fft.ifft(total, axis=1)[:, :E]
    factor = 1.0 / math.sqrt(NK * E)
    return (jnp.stack([-jnp.imag(corr), jnp.real(corr)], axis=1) * factor).astype(jnp.float32)

def reference(lesser, greater, coulomb, tile_block, shift_table):
    width = min(NNZ, 4096)
    count = NNZ // width

    def one(index):
        return polar_columns(lesser, greater, shift_table, index * width, width)
    parts = lax.map(one, jnp.arange(count, dtype=jnp.int32))
    polar_full = jnp.transpose(parts, (1, 2, 3, 0, 4)).reshape(NK, 2, E, NNZ)
    polarization = polar_full.astype(jnp.bfloat16)
    leading = polarization[:, :, :E // 4].reshape(NK, 2, E // 4, NT, BS, BS)
    inverse = jnp.argsort(tile_block).astype(jnp.int32)
    ordered = jnp.take(leading, inverse, axis=3).astype(jnp.float32)
    weights = coulomb.astype(jnp.float32)
    results = []
    for r, c in pattern_blocks(NBW):
        acc = jnp.zeros((NK, 2, E // 4, BS, BS), jnp.float32)
        for l in range(max(0, r - 1), min(NBW, r + 2)):
            if abs(l - c) <= 1:
                acc = acc + jnp.einsum('qij,qsejk->qseik', weights[:, 2 * r + l], ordered[:, :, :, 2 * l + c])
        results.append(acc)
    screened = jnp.stack(results, axis=3).reshape(NK, 2, E // 4, NNZ)
    return (polarization, screened)
```

```python
import math

import jax
import jax.numpy as jnp
import numpy as np
from jax import lax
from jax.experimental import pallas as pl
from jax.experimental.pallas import tpu as pltpu
from jax.sharding import PartitionSpec as P

E = 512
L = 128
FREQ = 2 * L
BLOCKS = E // L
CHIPS = 128
NNZ = 65536
PART = 128
MESH = pl.DeviceIdType.MESH


def split(table):
    high = table.astype(jnp.bfloat16)
    low = (table - high.astype(np.float64)).astype(jnp.bfloat16)
    return np.stack([high, low])


def tables():
    freq = np.concatenate([np.arange(0, FREQ, 2), np.arange(1, FREQ, 2)])
    angle = 2.0 * np.pi / FREQ * ((freq[:, None] * np.arange(L)[None, :]) % FREQ)
    cos, sin = np.cos(angle), np.sin(angle)
    forward = np.block([[cos, sin], [-sin, cos]])
    scale = 1.0 / (math.sqrt(2 * E) * FREQ)
    inverse = np.block([[-sin.T, -cos.T], [cos.T, -sin.T]]) * scale
    return split(forward), split(inverse)


def dot(a, b):
    return jnp.dot(a, b, preferred_element_type=jnp.float32)


def forward(got, b, tf, spec):
    @pl.loop(0, 8)
    def _(step):
        g, k, pair = step // 4, (step // 2) % 2, step % 2
        halves = []
        for h in range(2):
            rows = pl.ds((pair * 2 + h) * 32, 32)
            parts = [got[b, g, s, k, rows].reshape(L, PART) for s in range(2)]
            halves.append(jnp.concatenate(parts, axis=0))
        data = jnp.concatenate(halves, axis=1)
        result = dot(tf[0], data) + dot(tf[1], data)
        for h in range(2):
            for part in range(2):
                spec[g, k, pair * 2 + h, part] = result[
                    part * FREQ : (part + 1) * FREQ, h * PART : (h + 1) * PART
                ]


def products(shift, spec, mix):
    for q in range(2):
        for odd in range(2):

            @pl.loop(0, L // 16)
            def _(tile):
                rows = pl.ds(pl.multiple_of(odd * L + tile * 16, 16), 16)
                total = [[None, None] for _ in range(BLOCKS)]

                def add(d, part, value):
                    old = total[d][part]
                    total[d][part] = value if old is None else old + value

                for k in range(2):
                    other = shift[q, k]
                    left = [[spec[0, k, a, part, rows] for part in range(2)] for a in range(BLOCKS)]
                    for c in range(BLOCKS):
                        right_re = spec[1, other, c, 0, rows]
                        right_im = spec[1, other, c, 1, rows]
                        for d in range(BLOCKS - c):
                            re, im = left[c + d]
                            add(d, 0, re * right_re + im * right_im)
                            add(d, 1, im * right_re - re * right_im)
                for d in range(BLOCKS):
                    for part in range(2):
                        value = total[d][part]
                        if d + 1 < BLOCKS:
                            nxt = total[d + 1][part]
                            value = value - nxt if odd else value + nxt
                        high = value.astype(jnp.bfloat16)
                        low = (value - high.astype(jnp.float32)).astype(jnp.bfloat16)
                        mix[0, q, d, part, rows] = high
                        mix[1, q, d, part, rows] = low


def backward(b, ti, mix, swap, polar, near):
    for q in range(2):
        for pair in range(2):
            datas = []
            for level in range(2):
                halves = [mix[level, q, pair * 2 + h].reshape(2 * FREQ, PART) for h in range(2)]
                datas.append(jnp.concatenate(halves, axis=1))
            result = dot(ti[0], datas[0]) + dot(ti[0], datas[1]) + dot(ti[1], datas[0])
            result = result.astype(jnp.bfloat16)
            for h in range(2):
                for s in range(2):
                    value = result[s * L : (s + 1) * L, h * PART : (h + 1) * PART]
                    polar[b, q, s, pl.ds((pair * 2 + h) * 32, 32)] = value.reshape(32, 4, PART)
            if pair == 0:
                value = dot(swap[...], result[:, :PART]).astype(jnp.bfloat16)
                near[q, :, b] = value.reshape(L, 2, PART)


def screening(tile_block, weights, got, out):
    place = []
    for label in range(4):
        where = jnp.int32(0)
        for t in range(1, 4):
            where = jnp.where(tile_block[t] == label, t, where)
        place.append(where)
    sides = []
    for l in range(2):
        tiles = [got[place[2 * l + c]].reshape(2 * L, PART) for c in range(2)]
        sides.append(jnp.concatenate(tiles, axis=1))
    data = jnp.concatenate(sides, axis=0)
    for r in range(2):
        result = dot(weights[r], data)
        for c in range(2):
            for s in range(2):
                out[s, 2 * r + c] = result[s * L : (s + 1) * L, c * PART : (c + 1) * PART]


def prepare(coulomb, weights, swap):
    row = lax.broadcasted_iota(jnp.int32, (2 * L, 2 * L), 0)
    col = lax.broadcasted_iota(jnp.int32, (2 * L, 2 * L), 1)
    swap[...] = jnp.where(col == (row % 2) * L + row // 2, 1.0, 0.0).astype(jnp.bfloat16)
    wide_row = lax.broadcasted_iota(jnp.int32, (L, 2 * L), 0)
    wide_col = lax.broadcasted_iota(jnp.int32, (L, 2 * L), 1)
    for s in range(2):
        spread = jnp.where(wide_col == 2 * wide_row + s, 1.0, 0.0).astype(jnp.bfloat16)
        for r in range(2):
            for l in range(2):
                weights[r, s * L : (s + 1) * L, l * 2 * L : (l + 1) * 2 * L] = dot(
                    coulomb[0, 2 * r + l], spread
                ).astype(jnp.bfloat16)


def zigzag(i, n):
    return (i % 2) * ((i + 1) // 2) + (1 - i % 2) * ((n - i // 2) % n)


def peer(me, t):
    z, y, x = me // 16, (me // 4) % 4, me % 4
    dz = zigzag(t % 8, 8)
    dy = zigzag((t // 8 + t) % 4, 4)
    dx = zigzag((t // 32 + t // 2) % 4, 4)
    return ((z + dz) % 8) * 16 + ((y + dy) % 4) * 4 + (x + dx) % 4


def kernel(
    shift,
    tile_block,
    lesser,
    greater,
    coulomb,
    tf_hbm,
    ti_hbm,
    pol_out,
    scr_out,
    src,
    got,
    spec,
    mix,
    polar,
    near,
    near_got,
    tf,
    ti,
    weights,
    swap,
    load_sem,
    in_send,
    in_recv,
    pol_send,
    pol_recv,
    near_send,
    near_recv,
):
    me = lax.axis_index("energy")
    core = lax.axis_index("mom")
    loads = [
        pltpu.make_async_copy(lesser.at[0], src.at[0], load_sem.at[0]),
        pltpu.make_async_copy(greater.at[0], src.at[1], load_sem.at[1]),
        pltpu.make_async_copy(tf_hbm, tf, load_sem.at[2]),
        pltpu.make_async_copy(ti_hbm, ti, load_sem.at[3]),
    ]
    for load in loads:
        load.start()

    barrier = pltpu.get_barrier_semaphore()

    def greet(c, m):
        pl.semaphore_signal(barrier, inc=1, device_id=(c, m), device_id_type=MESH)

    greet(me, 1 - core)

    @pl.loop(1, CHIPS)
    def _(t):
        c = peer(me, t)
        greet(c, core)
        greet(c, 1 - core)

    prepare(coulomb, weights, swap)
    for load in loads:
        load.wait()
    pl.semaphore_wait(barrier, 2 * CHIPS - 1)

    def everyone(remote, local):
        local()
        remote(me, 1 - core)

        @pl.loop(1, CHIPS)
        def _(t):
            c = peer(me, t)
            remote(c, core)
            remote(c, 1 - core)

    def send_in(b):
        def ends(c, m):
            column = pl.multiple_of((c * 2 + m) * 2 * PART + b * PART, PART)
            return src.at[:, :, :, pl.ds(column, PART)], got.at[b, :, :, core, me]

        def remote(c, m):
            a, z = ends(c, m)
            pltpu.make_async_remote_copy(
                a, z, in_send.at[b], in_recv.at[b], device_id=(c, m), device_id_type=MESH
            ).start()

        def local():
            a, z = ends(me, core)
            pltpu.make_async_copy(a, z, in_recv.at[b]).start()

        everyone(remote, local)

    def send_pol(b):
        column = pl.multiple_of((me * 2 + core) * 2 * PART + b * PART, PART)

        def ends(c, m):
            return polar.at[b, m, :, c], pol_out.at[0, :, :, pl.ds(column, PART)]

        def remote(c, m):
            a, z = ends(c, m)
            pltpu.make_async_remote_copy(
                a, z, pol_send.at[b], pol_recv, device_id=(c, m), device_id_type=MESH
            ).start()

        def local():
            a, z = ends(me, core)
            pltpu.make_async_copy(a, z, pol_recv).start()

        everyone(remote, local)

    def send_near():
        def ends(c, m):
            return near.at[m, c], near_got.at[me // 32, me % 32, core]

        def remote(c, m):
            a, z = ends(c, m)
            pltpu.make_async_remote_copy(
                a, z, near_send, near_recv, device_id=(c, m), device_id_type=MESH
            ).start()

        def local():
            a, z = ends(me, core)
            pltpu.make_async_copy(a, z, near_recv).start()

        everyone(remote, local)

    def wait_all(ref, sem):
        pltpu.make_async_copy(ref, ref, sem).wait()

    sent = pl.ds(0, (2 * CHIPS - 1) * PART)
    for b in range(2):
        send_in(b)
    for b in range(2):
        wait_all(got.at[b], in_recv.at[b])
        forward(got, b, tf, spec)
        products(shift, spec, mix)
        backward(b, ti, mix, swap, polar, near)
        if b == 1:
            send_near()
        send_pol(b)
    wait_all(near_got, near_recv)
    screening(tile_block, weights, near_got, scr_out)
    wait_all(pol_out, pol_recv)
    for b in range(2):
        wait_all(src.at[:, :, :, sent], in_send.at[b])
        wait_all(src.at[0, :, :, sent], pol_send.at[b])
    wait_all(src.at[0, 0, :, sent], near_send)


def shards(lesser, greater, coulomb, tile_block, shift_table):
    tf, ti = tables()
    bf16, f32 = jnp.bfloat16, jnp.float32
    hbm = pl.BlockSpec(memory_space=pl.ANY)
    smem = pl.BlockSpec(memory_space=pltpu.SMEM)
    vmem = pl.BlockSpec(memory_space=pltpu.VMEM)
    polarization, screened = pl.pallas_call(
        kernel,
        out_shape=(
            jax.ShapeDtypeStruct((1, 2, E // CHIPS, NNZ), bf16),
            jax.ShapeDtypeStruct((2, 4, L, PART), f32),
        ),
        in_specs=[smem, smem, hbm, hbm, vmem, hbm, hbm],
        out_specs=(hbm, vmem),
        scratch_shapes=[
            pltpu.VMEM((2, 2, E // CHIPS, NNZ), bf16),
            pltpu.VMEM((2, 2, 2, 2, CHIPS, E // CHIPS, PART), bf16),
            pltpu.VMEM((2, 2, BLOCKS, 2, FREQ, PART), f32),
            pltpu.VMEM((2, 2, BLOCKS, 2, FREQ, PART), bf16),
            pltpu.VMEM((2, 2, 2, CHIPS, E // CHIPS, PART), bf16),
            pltpu.VMEM((2, L, 2, 2, PART), bf16),
            pltpu.VMEM((4, 32, 2, 2, 2, PART), bf16),
            pltpu.VMEM((2, 2 * FREQ, 2 * L), bf16),
            pltpu.VMEM((2, 2 * L, 2 * FREQ), bf16),
            pltpu.VMEM((2, 2 * L, 4 * L), bf16),
            pltpu.VMEM((2 * L, 2 * L), bf16),
            pltpu.SemaphoreType.DMA((4,)),
            pltpu.SemaphoreType.DMA((2,)),
            pltpu.SemaphoreType.DMA((2,)),
            pltpu.SemaphoreType.DMA((2,)),
            pltpu.SemaphoreType.DMA,
            pltpu.SemaphoreType.DMA,
            pltpu.SemaphoreType.DMA,
        ],
        compiler_params=pltpu.CompilerParams(
            collective_id=0, has_side_effects=True, vmem_limit_bytes=48 << 20
        ),
        name="polarization",
    )(shift_table, tile_block, lesser, greater, coulomb, jnp.asarray(tf), jnp.asarray(ti))
    return (polarization, screened.reshape(1, 2, 1, NNZ))


def solution(mesh):
    return jax.shard_map(
        shards,
        mesh=mesh,
        in_specs=(
            P("mom", None, "energy", None),
            P("mom", None, "energy", None),
            P("mom", None, None, None),
            P(),
            P(),
        ),
        out_specs=(P("mom", None, "energy", None), P("mom", None, "energy", None)),
        check_vma=False,
    )
```

```python
import math

import jax
import jax.numpy as jnp
import numpy as np
from jax import lax
from jax.experimental import pallas as pl
from jax.experimental.pallas import tpu as pltpu
from jax.sharding import PartitionSpec as P

E = 512
L = 128
FREQ = 2 * L
BLOCKS = E // L
CHIPS = 128
NNZ = 65536
PART = 128
MESH = pl.DeviceIdType.MESH


def split(table):
    high = table.astype(jnp.bfloat16)
    low = (table - high.astype(np.float64)).astype(jnp.bfloat16)
    return np.stack([high, low])


def tables():
    freq = np.concatenate([np.arange(0, FREQ, 2), np.arange(1, FREQ, 2)])
    angle = 2.0 * np.pi / FREQ * ((freq[:, None] * np.arange(L)[None, :]) % FREQ)
    cos, sin = np.cos(angle), np.sin(angle)
    forward = np.block([[cos, sin], [-sin, cos]])
    scale = 1.0 / (math.sqrt(2 * E) * FREQ)
    inverse = np.block([[-sin.T, -cos.T], [cos.T, -sin.T]]) * scale
    return split(forward), split(inverse)


def dot(a, b):
    return jnp.dot(a, b, preferred_element_type=jnp.float32)


def forward(got, b, tf, spec):
    @pl.loop(0, 8)
    def _(step):
        g, k, pair = step // 4, (step // 2) % 2, step % 2
        halves = []
        for h in range(2):
            rows = pl.ds((pair * 2 + h) * 32, 32)
            parts = [got[b, g, s, k, rows].reshape(L, PART) for s in range(2)]
            halves.append(jnp.concatenate(parts, axis=0))
        data = jnp.concatenate(halves, axis=1)
        result = dot(tf[0], data) + dot(tf[1], data)
        for h in range(2):
            for part in range(2):
                spec[g, k, pair * 2 + h, part] = result[
                    part * FREQ : (part + 1) * FREQ, h * PART : (h + 1) * PART
                ]


def products(q, shift, spec, mix):
    for odd in range(2):

        @pl.loop(0, L // 16)
        def _(tile):
            rows = pl.ds(pl.multiple_of(odd * L + tile * 16, 16), 16)
            total = [[None, None] for _ in range(BLOCKS)]

            def add(d, part, value):
                old = total[d][part]
                total[d][part] = value if old is None else old + value

            for k in range(2):
                other = shift[q, k]
                left = [[spec[0, k, a, part, rows] for part in range(2)] for a in range(BLOCKS)]
                for c in range(BLOCKS):
                    right_re = spec[1, other, c, 0, rows]
                    right_im = spec[1, other, c, 1, rows]
                    for d in range(BLOCKS - c):
                        re, im = left[c + d]
                        add(d, 0, re * right_re + im * right_im)
                        add(d, 1, im * right_re - re * right_im)
            for d in range(BLOCKS):
                for part in range(2):
                    value = total[d][part]
                    if d + 1 < BLOCKS:
                        nxt = total[d + 1][part]
                        value = value - nxt if odd else value + nxt
                    high = value.astype(jnp.bfloat16)
                    low = (value - high.astype(jnp.float32)).astype(jnp.bfloat16)
                    mix[0, q, d, part, rows] = high
                    mix[1, q, d, part, rows] = low


def backward(b, ti, mix, swap, polar, near):
    for q in range(2):
        for pair in range(2):
            datas = []
            for level in range(2):
                halves = [mix[level, q, pair * 2 + h].reshape(2 * FREQ, PART) for h in range(2)]
                datas.append(jnp.concatenate(halves, axis=1))
            result = dot(ti[0], datas[0]) + dot(ti[0], datas[1]) + dot(ti[1], datas[0])
            result = result.astype(jnp.bfloat16)
            for h in range(2):
                for s in range(2):
                    value = result[s * L : (s + 1) * L, h * PART : (h + 1) * PART]
                    polar[b, q, s, pl.ds((pair * 2 + h) * 32, 32)] = value.reshape(32, 4, PART)
            if pair == 0:
                value = dot(swap[...], result[:, :PART]).astype(jnp.bfloat16)
                near[q, :, b] = value.reshape(L, 2, PART)


def screening(tile_block, weights, got, out):
    place = []
    for label in range(4):
        where = jnp.int32(0)
        for t in range(1, 4):
            where = jnp.where(tile_block[t] == label, t, where)
        place.append(where)
    sides = []
    for l in range(2):
        tiles = [got[place[2 * l + c]].reshape(2 * L, PART) for c in range(2)]
        sides.append(jnp.concatenate(tiles, axis=1))
    data = jnp.concatenate(sides, axis=0)
    for r in range(2):
        result = dot(weights[r], data)
        for c in range(2):
            for s in range(2):
                out[s, 2 * r + c] = result[s * L : (s + 1) * L, c * PART : (c + 1) * PART]


def prepare(coulomb, weights, swap):
    row = lax.broadcasted_iota(jnp.int32, (2 * L, 2 * L), 0)
    col = lax.broadcasted_iota(jnp.int32, (2 * L, 2 * L), 1)
    swap[...] = jnp.where(col == (row % 2) * L + row // 2, 1.0, 0.0).astype(jnp.bfloat16)
    wide_row = lax.broadcasted_iota(jnp.int32, (L, 2 * L), 0)
    wide_col = lax.broadcasted_iota(jnp.int32, (L, 2 * L), 1)
    for s in range(2):
        spread = jnp.where(wide_col == 2 * wide_row + s, 1.0, 0.0).astype(jnp.bfloat16)
        for r in range(2):
            for l in range(2):
                weights[r, s * L : (s + 1) * L, l * 2 * L : (l + 1) * 2 * L] = dot(
                    coulomb[0, 2 * r + l], spread
                ).astype(jnp.bfloat16)


def place():
    me = lax.axis_index("energy")
    return lax.div(me, 16), lax.rem(lax.div(me, 4), 4), lax.rem(me, 4)


def chip(z, y, x):
    return z * 16 + y * 4 + x


def greet_all(barrier, ready):
    core = lax.axis_index("mom")
    z, y, x = place()

    def plane(sem):
        @pl.loop(1, 16)
        def _(t):
            c = chip(z, lax.rem(y + lax.div(t, 4), 4), lax.rem(x + lax.rem(t, 4), 4))
            pl.semaphore_signal(sem, inc=1, device_id=(c, core), device_id_type=MESH)

    plane(barrier)
    pl.semaphore_signal(barrier, inc=1, device_id=(chip(z, y, x), 1 - core), device_id_type=MESH)

    @pl.loop(1, 8)
    def _(t):
        c = chip(lax.rem(z + t, 8), y, x)
        for m in range(2):
            pl.semaphore_signal(barrier, inc=1, device_id=(c, m), device_id_type=MESH)

    pl.semaphore_wait(barrier, 30)
    plane(ready)
    pl.semaphore_wait(ready, 15)


def peers(group, act):
    core = lax.axis_index("mom")
    z, y, x = place()
    for i, dz in enumerate((0, 1, 7, 2, 6, 3, 5, 4)):
        row = lax.rem(y + group + i, 4)
        col = lax.rem(x + lax.div(jnp.int32(group), 4) + i // 2, 4)
        c = chip(lax.rem(z + dz, 8), row, col)
        if not (isinstance(group, int) and group == 0 and i == 0):
            act(c, core)
        act(c, 1 - core)


def send(first, last, remote, local):
    if first == 0:
        local()
        peers(0, remote)
        first = 1

    @pl.loop(first, last)
    def _(group):
        peers(group, remote)


def kernel(
    shift,
    tile_block,
    lesser,
    greater,
    coulomb,
    tf_hbm,
    ti_hbm,
    pol_out,
    scr_out,
    src,
    got,
    spec,
    mix,
    polar,
    near,
    near_got,
    tf,
    ti,
    weights,
    swap,
    ready,
    load_sem,
    in_send,
    in_recv,
    pol_send,
    pol_recv,
    near_send,
    near_recv,
):
    me = lax.axis_index("energy")
    core = lax.axis_index("mom")
    loads = [
        pltpu.make_async_copy(lesser.at[0], src.at[0], load_sem.at[0]),
        pltpu.make_async_copy(greater.at[0], src.at[1], load_sem.at[1]),
        pltpu.make_async_copy(tf_hbm, tf, load_sem.at[2]),
        pltpu.make_async_copy(ti_hbm, ti, load_sem.at[3]),
    ]
    for load in loads:
        load.start()

    barrier = pltpu.get_barrier_semaphore()
    greet_all(barrier, ready)
    for load in loads[:2]:
        load.wait()

    def send_in(b, first, last):
        def ends(c, m):
            column = pl.multiple_of((c * 2 + m) * 2 * PART + b * PART, PART)
            return src.at[:, :, :, pl.ds(column, PART)], got.at[b, :, :, core, me]

        def remote(c, m):
            a, z = ends(c, m)
            pltpu.make_async_remote_copy(
                a, z, in_send.at[b], in_recv.at[b], device_id=(c, m), device_id_type=MESH
            ).start()

        def local():
            a, z = ends(me, core)
            pltpu.make_async_copy(a, z, in_recv.at[b]).start()

        send(first, last, remote, local)

    def send_pol(b, first, last):
        column = pl.multiple_of((me * 2 + core) * 2 * PART + b * PART, PART)

        def ends(c, m):
            return polar.at[b, m, :, c], pol_out.at[0, :, :, pl.ds(column, PART)]

        def remote(c, m):
            a, z = ends(c, m)
            pltpu.make_async_remote_copy(
                a, z, pol_send.at[b], pol_recv, device_id=(c, m), device_id_type=MESH
            ).start()

        def local():
            a, z = ends(me, core)
            pltpu.make_async_copy(a, z, pol_recv).start()

        send(first, last, remote, local)

    def send_near():
        def ends(c, m):
            return near.at[m, c], near_got.at[me // 32, me % 32, core]

        def remote(c, m):
            a, z = ends(c, m)
            pltpu.make_async_remote_copy(
                a, z, near_send, near_recv, device_id=(c, m), device_id_type=MESH
            ).start()

        def local():
            a, z = ends(me, core)
            pltpu.make_async_copy(a, z, near_recv).start()

        send(0, 16, remote, local)

    def wait_all(ref, sem):
        pltpu.make_async_copy(ref, ref, sem).wait()

    def compute(b):
        forward(got, b, tf, spec)
        for q in range(2):
            products(q, shift, spec, mix)
        backward(b, ti, mix, swap, polar, near)

    sent = pl.ds(0, (2 * CHIPS - 1) * PART)
    send_in(0, 0, 16)
    send_in(1, 0, 16)
    prepare(coulomb, weights, swap)
    for load in loads[2:]:
        load.wait()
    wait_all(got.at[0], in_recv.at[0])
    compute(0)
    send_pol(0, 0, 16)
    wait_all(got.at[1], in_recv.at[1])
    compute(1)
    send_near()
    send_pol(1, 0, 16)
    wait_all(near_got, near_recv)
    screening(tile_block, weights, near_got, scr_out)
    wait_all(pol_out, pol_recv)
    for b in range(2):
        wait_all(src.at[:, :, :, sent], in_send.at[b])
        wait_all(src.at[0, :, :, sent], pol_send.at[b])
    wait_all(src.at[0, 0, :, sent], near_send)


def shards(lesser, greater, coulomb, tile_block, shift_table):
    tf, ti = tables()
    bf16, f32 = jnp.bfloat16, jnp.float32
    hbm = pl.BlockSpec(memory_space=pl.ANY)
    smem = pl.BlockSpec(memory_space=pltpu.SMEM)
    vmem = pl.BlockSpec(memory_space=pltpu.VMEM)
    operands = (shift_table, tile_block, lesser, greater, coulomb, jnp.asarray(tf), jnp.asarray(ti))
    polarization, screened = pl.pallas_call(
        kernel,
        out_shape=(
            jax.ShapeDtypeStruct((1, 2, E // CHIPS, NNZ), bf16),
            jax.ShapeDtypeStruct((2, 4, L, PART), f32),
        ),
        in_specs=[smem, smem, hbm, hbm, vmem, hbm, hbm],
        out_specs=(hbm, vmem),
        scratch_shapes=[
            pltpu.VMEM((2, 2, E // CHIPS, NNZ), bf16),
            pltpu.VMEM((2, 2, 2, 2, CHIPS, E // CHIPS, PART), bf16),
            pltpu.VMEM((2, 2, BLOCKS, 2, FREQ, PART), f32),
            pltpu.VMEM((2, 2, BLOCKS, 2, FREQ, PART), bf16),
            pltpu.VMEM((2, 2, 2, CHIPS, E // CHIPS, PART), bf16),
            pltpu.VMEM((2, L, 2, 2, PART), bf16),
            pltpu.VMEM((4, 32, 2, 2, 2, PART), bf16),
            pltpu.VMEM((2, 2 * FREQ, 2 * L), bf16),
            pltpu.VMEM((2, 2 * L, 2 * FREQ), bf16),
            pltpu.VMEM((2, 2 * L, 4 * L), bf16),
            pltpu.VMEM((2 * L, 2 * L), bf16),
            pltpu.SemaphoreType.REGULAR,
            pltpu.SemaphoreType.DMA((4,)),
            pltpu.SemaphoreType.DMA((2,)),
            pltpu.SemaphoreType.DMA((2,)),
            pltpu.SemaphoreType.DMA((2,)),
            pltpu.SemaphoreType.DMA,
            pltpu.SemaphoreType.DMA,
            pltpu.SemaphoreType.DMA,
        ],
        compiler_params=pltpu.CompilerParams(
            collective_id=0, has_side_effects=True, vmem_limit_bytes=48 << 20
        ),
        name="polarization",
    )(*(pltpu.with_memory_space_constraint(operand, pltpu.HBM) for operand in operands))
    return (polarization, screened.reshape(1, 2, 1, NNZ))


def solution(mesh):
    return jax.shard_map(
        shards,
        mesh=mesh,
        in_specs=(
            P("mom", None, "energy", None),
            P("mom", None, "energy", None),
            P("mom", None, None, None),
            P(),
            P(),
        ),
        out_specs=(P("mom", None, "energy", None), P("mom", None, "energy", None)),
        check_vma=False,
    )
```

```python
import functools
import math

import jax
import jax.numpy as jnp
import numpy as np
from jax import lax
from jax.experimental import pallas as pl
from jax.experimental.pallas import tpu as pltpu
from jax.sharding import PartitionSpec as P

E = 512
L = 128
FREQ = 2 * L
BLOCKS = E // L
CHIPS = 128
NNZ = 65536
PART = 128
MESH = pl.DeviceIdType.MESH


def split(table):
    high = table.astype(jnp.bfloat16)
    low = (table - high.astype(np.float64)).astype(jnp.bfloat16)
    return np.stack([high, low])


def tables():
    freq = np.concatenate([np.arange(0, FREQ, 2), np.arange(1, FREQ, 2)])
    angle = 2.0 * np.pi / FREQ * ((freq[:, None] * np.arange(L)[None, :]) % FREQ)
    cos, sin = np.cos(angle), np.sin(angle)
    forward = np.block([[cos, sin], [-sin, cos]])
    scale = 1.0 / (math.sqrt(2 * E) * FREQ)
    inverse = np.block([[-sin.T, -cos.T], [cos.T, -sin.T]]) * scale
    return split(forward), split(inverse)


def dot(a, b):
    return jnp.dot(a, b, preferred_element_type=jnp.float32)


def forward(got, b, tf, spec):
    @pl.loop(0, 8)
    def _(step):
        g, k, pair = step // 4, (step // 2) % 2, step % 2
        halves = []
        for h in range(2):
            rows = pl.ds((pair * 2 + h) * 32, 32)
            parts = [got[b, g, s, k, rows].reshape(L, PART) for s in range(2)]
            halves.append(jnp.concatenate(parts, axis=0))
        data = jnp.concatenate(halves, axis=1)
        result = dot(tf[0], data) + dot(tf[1], data)
        for h in range(2):
            for part in range(2):
                spec[g, k, pair * 2 + h, part] = result[
                    part * FREQ : (part + 1) * FREQ, h * PART : (h + 1) * PART
                ]


def products(q, shift, spec, mix):
    for odd in range(2):

        @pl.loop(0, L // 16)
        def _(tile):
            rows = pl.ds(pl.multiple_of(odd * L + tile * 16, 16), 16)
            total = [[None, None] for _ in range(BLOCKS)]

            def add(d, part, value):
                old = total[d][part]
                total[d][part] = value if old is None else old + value

            for k in range(2):
                other = shift[q, k]
                left = [[spec[0, k, a, part, rows] for part in range(2)] for a in range(BLOCKS)]
                for c in range(BLOCKS):
                    right_re = spec[1, other, c, 0, rows]
                    right_im = spec[1, other, c, 1, rows]
                    for d in range(BLOCKS - c):
                        re, im = left[c + d]
                        add(d, 0, re * right_re + im * right_im)
                        add(d, 1, im * right_re - re * right_im)
            for d in range(BLOCKS):
                for part in range(2):
                    value = total[d][part]
                    if d + 1 < BLOCKS:
                        nxt = total[d + 1][part]
                        value = value - nxt if odd else value + nxt
                    high = value.astype(jnp.bfloat16)
                    low = (value - high.astype(jnp.float32)).astype(jnp.bfloat16)
                    mix[0, q, d, part, rows] = high
                    mix[1, q, d, part, rows] = low


def backward(q, b, ti, mix, swap, polar, near):
    for pair in range(2):
        datas = []
        for level in range(2):
            halves = [mix[level, q, pair * 2 + h].reshape(2 * FREQ, PART) for h in range(2)]
            datas.append(jnp.concatenate(halves, axis=1))
        result = dot(ti[0], datas[0]) + dot(ti[0], datas[1]) + dot(ti[1], datas[0])
        result = result.astype(jnp.bfloat16)
        for h in range(2):
            for s in range(2):
                value = result[s * L : (s + 1) * L, h * PART : (h + 1) * PART]
                polar[b, q, s, pl.ds((pair * 2 + h) * 32, 32)] = value.reshape(32, 4, PART)
        if pair == 0:
            value = dot(swap[...], result[:, :PART]).astype(jnp.bfloat16)
            near[q, :, b] = value.reshape(L, 2, PART)


def screening(tile_block, weights, got, out):
    place = []
    for label in range(4):
        where = jnp.int32(0)
        for t in range(1, 4):
            where = jnp.where(tile_block[t] == label, t, where)
        place.append(where)
    sides = []
    for l in range(2):
        tiles = [got[place[2 * l + c]].reshape(2 * L, PART) for c in range(2)]
        sides.append(jnp.concatenate(tiles, axis=1))
    data = jnp.concatenate(sides, axis=0)
    for r in range(2):
        result = dot(weights[r], data)
        for c in range(2):
            for s in range(2):
                out[s, 2 * r + c] = result[s * L : (s + 1) * L, c * PART : (c + 1) * PART]


def prepare(coulomb, weights, swap):
    row = lax.broadcasted_iota(jnp.int32, (2 * L, 2 * L), 0)
    col = lax.broadcasted_iota(jnp.int32, (2 * L, 2 * L), 1)
    swap[...] = jnp.where(col == (row % 2) * L + row // 2, 1.0, 0.0).astype(jnp.bfloat16)
    wide_row = lax.broadcasted_iota(jnp.int32, (L, 2 * L), 0)
    wide_col = lax.broadcasted_iota(jnp.int32, (L, 2 * L), 1)
    for s in range(2):
        spread = jnp.where(wide_col == 2 * wide_row + s, 1.0, 0.0).astype(jnp.bfloat16)
        for r in range(2):
            for l in range(2):
                weights[r, s * L : (s + 1) * L, l * 2 * L : (l + 1) * 2 * L] = dot(
                    coulomb[0, 2 * r + l], spread
                ).astype(jnp.bfloat16)


def place():
    me = lax.axis_index("energy")
    return lax.div(me, 16), lax.rem(lax.div(me, 4), 4), lax.rem(me, 4)


def chip(z, y, x):
    return z * 16 + y * 4 + x


def greet(barrier, ready):
    core = lax.axis_index("mom")
    z, y, x = place()

    def plane(sem):
        @pl.loop(1, 16)
        def _(t):
            c = chip(z, lax.rem(y + lax.div(t, 4), 4), lax.rem(x + lax.rem(t, 4), 4))
            pl.semaphore_signal(sem, inc=1, device_id=(c, core), device_id_type=MESH)

    plane(barrier)
    pl.semaphore_signal(barrier, inc=1, device_id=(chip(z, y, x), 1 - core), device_id_type=MESH)

    @pl.loop(1, 8)
    def _(t):
        c = chip(lax.rem(z + t, 8), y, x)
        for m in range(2):
            pl.semaphore_signal(barrier, inc=1, device_id=(c, m), device_id_type=MESH)

    pl.semaphore_wait(barrier, 30)
    plane(ready)


STEPS = (0, 1, 7, 2, 6, 3, 5, 4)


def line(act):
    core = lax.axis_index("mom")
    z, y, x = place()
    act(chip(z, y, x), 1 - core)
    for dz in STEPS[1:]:
        c = chip(lax.rem(z + dz, 8), y, x)
        act(c, core)
        act(c, 1 - core)


def others(act):
    z, y, x = place()

    @pl.loop(0, 16)
    def _(group):
        for i, dz in enumerate(STEPS):
            own = (-(i // 2)) % 4 * 4 + (-i) % 4

            @pl.when(group != own)
            def _():
                row = lax.rem(y + group + i, 4)
                col = lax.rem(x + lax.div(group, 4) + i // 2, 4)
                act(chip(lax.rem(z + dz, 8), row, col))


def both_cores(remote, core, c):
    remote(c, core)
    remote(c, 1 - core)


def send(remote, local):
    core = lax.axis_index("mom")
    local()
    line(remote)
    others(functools.partial(both_cores, remote, core))


def send_to(q, remote, local):
    core = lax.axis_index("mom")
    z, y, x = place()

    @pl.when(core == q)
    def _():
        local()

    @pl.when(core != q)
    def _():
        remote(chip(z, y, x), q)

    for dz in STEPS[1:]:
        remote(chip(lax.rem(z + dz, 8), y, x), q)
    others(lambda c: remote(c, q))


def kernel(
    shift,
    tile_block,
    lesser,
    greater,
    coulomb,
    tf_hbm,
    ti_hbm,
    pol_out,
    scr_out,
    src,
    got,
    spec,
    mix,
    polar,
    near,
    near_got,
    tf,
    ti,
    weights,
    swap,
    ready,
    load_sem,
    in_send,
    in_recv,
    pol_send,
    pol_recv,
    near_send,
    near_recv,
):
    me = lax.axis_index("energy")
    core = lax.axis_index("mom")
    loads = [
        pltpu.make_async_copy(lesser.at[0], src.at[0], load_sem.at[0]),
        pltpu.make_async_copy(greater.at[0], src.at[1], load_sem.at[1]),
        pltpu.make_async_copy(tf_hbm, tf, load_sem.at[2]),
        pltpu.make_async_copy(ti_hbm, ti, load_sem.at[3]),
    ]
    for load in loads:
        load.start()

    barrier = pltpu.get_barrier_semaphore()
    greet(barrier, ready)
    for load in loads[:2]:
        load.wait()

    def copies(source, target, send_sem, recv_sem):
        def remote(c, m):
            pltpu.make_async_remote_copy(
                source(c, m), target, send_sem, recv_sem, device_id=(c, m), device_id_type=MESH
            ).start()

        def local():
            pltpu.make_async_copy(source(me, core), target, recv_sem).start()

        return remote, local

    def copies_in(b):
        def source(c, m):
            column = pl.multiple_of((c * 2 + m) * 2 * PART + b * PART, PART)
            return src.at[:, :, :, pl.ds(column, PART)]

        return copies(source, got.at[b, :, :, core, me], in_send.at[b], in_recv.at[b])

    def copies_pol(b):
        column = pl.multiple_of((me * 2 + core) * 2 * PART + b * PART, PART)
        return copies(
            lambda c, m: polar.at[b, m, :, c],
            pol_out.at[0, :, :, pl.ds(column, PART)],
            pol_send.at[b],
            pol_recv,
        )

    def copies_near():
        place_of = near_got.at[lax.div(me, 32), lax.rem(me, 32), core]
        return copies(lambda c, m: near.at[m, c], place_of, near_send, near_recv)

    def wait_all(ref, sem):
        pltpu.make_async_copy(ref, ref, sem).wait()

    sent = pl.ds(0, (2 * CHIPS - 1) * PART)
    for b in range(2):
        remote, local = copies_in(b)
        line(remote)
        local()
    pl.semaphore_wait(ready, 15)
    for b in range(2):
        remote, _ = copies_in(b)
        others(functools.partial(both_cores, remote, core))
    prepare(coulomb, weights, swap)
    for load in loads[2:]:
        load.wait()
    for b in range(2):
        wait_all(got.at[b], in_recv.at[b])
        forward(got, b, tf, spec)
        for q in range(2):
            products(q, shift, spec, mix)
            backward(q, b, ti, mix, swap, polar, near)
            if b == 1:
                send_to(q, *copies_near())
                send_to(q, *copies_pol(b))
        if b == 0:
            send(*copies_pol(b))
    wait_all(near_got, near_recv)
    screening(tile_block, weights, near_got, scr_out)
    wait_all(pol_out, pol_recv)
    for b in range(2):
        wait_all(src.at[:, :, :, sent], in_send.at[b])
        wait_all(src.at[0, :, :, sent], pol_send.at[b])
    wait_all(src.at[0, 0, :, sent], near_send)


def shards(lesser, greater, coulomb, tile_block, shift_table):
    tf, ti = tables()
    bf16, f32 = jnp.bfloat16, jnp.float32
    hbm = pl.BlockSpec(memory_space=pl.ANY)
    smem = pl.BlockSpec(memory_space=pltpu.SMEM)
    vmem = pl.BlockSpec(memory_space=pltpu.VMEM)
    operands = (shift_table, tile_block, lesser, greater, coulomb, jnp.asarray(tf), jnp.asarray(ti))
    polarization, screened = pl.pallas_call(
        kernel,
        out_shape=(
            jax.ShapeDtypeStruct((1, 2, E // CHIPS, NNZ), bf16),
            jax.ShapeDtypeStruct((2, 4, L, PART), f32),
        ),
        in_specs=[smem, smem, hbm, hbm, vmem, hbm, hbm],
        out_specs=(hbm, vmem),
        scratch_shapes=[
            pltpu.VMEM((2, 2, E // CHIPS, NNZ), bf16),
            pltpu.VMEM((2, 2, 2, 2, CHIPS, E // CHIPS, PART), bf16),
            pltpu.VMEM((2, 2, BLOCKS, 2, FREQ, PART), f32),
            pltpu.VMEM((2, 2, BLOCKS, 2, FREQ, PART), bf16),
            pltpu.VMEM((2, 2, 2, CHIPS, E // CHIPS, PART), bf16),
            pltpu.VMEM((2, L, 2, 2, PART), bf16),
            pltpu.VMEM((4, 32, 2, 2, 2, PART), bf16),
            pltpu.VMEM((2, 2 * FREQ, 2 * L), bf16),
            pltpu.VMEM((2, 2 * L, 2 * FREQ), bf16),
            pltpu.VMEM((2, 2 * L, 4 * L), bf16),
            pltpu.VMEM((2 * L, 2 * L), bf16),
            pltpu.SemaphoreType.REGULAR,
            pltpu.SemaphoreType.DMA((4,)),
            pltpu.SemaphoreType.DMA((2,)),
            pltpu.SemaphoreType.DMA((2,)),
            pltpu.SemaphoreType.DMA((2,)),
            pltpu.SemaphoreType.DMA,
            pltpu.SemaphoreType.DMA,
            pltpu.SemaphoreType.DMA,
        ],
        compiler_params=pltpu.CompilerParams(
            collective_id=0, has_side_effects=True, vmem_limit_bytes=48 << 20
        ),
        name="polarization",
    )(*(pltpu.with_memory_space_constraint(operand, pltpu.HBM) for operand in operands))
    return (polarization, screened.reshape(1, 2, 1, NNZ))


def solution(mesh):
    return jax.shard_map(
        shards,
        mesh=mesh,
        in_specs=(
            P("mom", None, "energy", None),
            P("mom", None, "energy", None),
            P("mom", None, None, None),
            P(),
            P(),
        ),
        out_specs=(P("mom", None, "energy", None), P("mom", None, "energy", None)),
        check_vma=False,
    )
```

```python
import functools
import math

import jax
import jax.numpy as jnp
import numpy as np
from jax import lax
from jax.experimental import pallas as pl
from jax.experimental.pallas import tpu as pltpu
from jax.sharding import PartitionSpec as P

E = 512
L = 128
FREQ = 2 * L
BLOCKS = E // L
CHIPS = 128
NNZ = 65536
PART = 128
MESH = pl.DeviceIdType.MESH


def split(table):
    high = table.astype(jnp.bfloat16)
    low = (table - high.astype(np.float64)).astype(jnp.bfloat16)
    return np.stack([high, low])


def tables():
    freq = np.concatenate([np.arange(0, FREQ, 2), np.arange(1, FREQ, 2)])
    angle = 2.0 * np.pi / FREQ * ((freq[:, None] * np.arange(L)[None, :]) % FREQ)
    cos, sin = np.cos(angle), np.sin(angle)
    forward = np.block([[cos, sin], [-sin, cos]])
    scale = 1.0 / (math.sqrt(2 * E) * FREQ)
    inverse = np.block([[-sin.T, -cos.T], [cos.T, -sin.T]]) * scale
    return split(forward), split(inverse)


def dot(a, b):
    return jnp.dot(a, b, preferred_element_type=jnp.float32)


def forward(got, b, tf, spec):
    @pl.loop(0, 8)
    def _(step):
        g, k, pair = step // 4, (step // 2) % 2, step % 2
        halves = []
        for h in range(2):
            rows = pl.ds((pair * 2 + h) * 32, 32)
            parts = [got[b, g, s, k, rows].reshape(L, PART) for s in range(2)]
            halves.append(jnp.concatenate(parts, axis=0))
        data = jnp.concatenate(halves, axis=1)
        result = dot(tf[0], data) + dot(tf[1], data)
        for h in range(2):
            for part in range(2):
                spec[g, k, pair * 2 + h, part] = result[
                    part * FREQ : (part + 1) * FREQ, h * PART : (h + 1) * PART
                ]


def products(q, shift, spec, mix):
    for odd in range(2):

        @pl.loop(0, L // 16)
        def _(tile):
            rows = pl.ds(pl.multiple_of(odd * L + tile * 16, 16), 16)
            total = [[None, None] for _ in range(BLOCKS)]

            def add(d, part, value):
                old = total[d][part]
                total[d][part] = value if old is None else old + value

            for k in range(2):
                other = shift[q, k]
                left = [[spec[0, k, a, part, rows] for part in range(2)] for a in range(BLOCKS)]
                for c in range(BLOCKS):
                    right_re = spec[1, other, c, 0, rows]
                    right_im = spec[1, other, c, 1, rows]
                    for d in range(BLOCKS - c):
                        re, im = left[c + d]
                        add(d, 0, re * right_re + im * right_im)
                        add(d, 1, im * right_re - re * right_im)
            for d in range(BLOCKS):
                for part in range(2):
                    value = total[d][part]
                    if d + 1 < BLOCKS:
                        nxt = total[d + 1][part]
                        value = value - nxt if odd else value + nxt
                    high = value.astype(jnp.bfloat16)
                    low = (value - high.astype(jnp.float32)).astype(jnp.bfloat16)
                    mix[0, q, d, part, rows] = high
                    mix[1, q, d, part, rows] = low


def backward(q, b, ti, mix, swap, polar, near):
    for pair in range(2):
        datas = []
        for level in range(2):
            halves = [mix[level, q, pair * 2 + h].reshape(2 * FREQ, PART) for h in range(2)]
            datas.append(jnp.concatenate(halves, axis=1))
        result = dot(ti[0], datas[0]) + dot(ti[0], datas[1]) + dot(ti[1], datas[0])
        result = result.astype(jnp.bfloat16)
        for h in range(2):
            for s in range(2):
                value = result[s * L : (s + 1) * L, h * PART : (h + 1) * PART]
                polar[b, q, s, pl.ds((pair * 2 + h) * 32, 32)] = value.reshape(32, 4, PART)
        if pair == 0:
            value = dot(swap[...], result[:, :PART]).astype(jnp.bfloat16)
            near[q, :, b] = value.reshape(L, 2, PART)


def screening(tile_block, weights, got, out):
    place = []
    for label in range(4):
        where = jnp.int32(0)
        for t in range(1, 4):
            where = jnp.where(tile_block[t] == label, t, where)
        place.append(where)
    sides = []
    for l in range(2):
        tiles = [got[place[2 * l + c]].reshape(2 * L, PART) for c in range(2)]
        sides.append(jnp.concatenate(tiles, axis=1))
    data = jnp.concatenate(sides, axis=0)
    for r in range(2):
        result = dot(weights[r], data)
        for c in range(2):
            for s in range(2):
                out[s, 2 * r + c] = result[s * L : (s + 1) * L, c * PART : (c + 1) * PART]


def prepare(coulomb, weights, swap):
    row = lax.broadcasted_iota(jnp.int32, (2 * L, 2 * L), 0)
    col = lax.broadcasted_iota(jnp.int32, (2 * L, 2 * L), 1)
    swap[...] = jnp.where(col == (row % 2) * L + row // 2, 1.0, 0.0).astype(jnp.bfloat16)
    wide_row = lax.broadcasted_iota(jnp.int32, (L, 2 * L), 0)
    wide_col = lax.broadcasted_iota(jnp.int32, (L, 2 * L), 1)
    for s in range(2):
        spread = jnp.where(wide_col == 2 * wide_row + s, 1.0, 0.0).astype(jnp.bfloat16)
        for r in range(2):
            for l in range(2):
                weights[r, s * L : (s + 1) * L, l * 2 * L : (l + 1) * 2 * L] = dot(
                    coulomb[0, 2 * r + l], spread
                ).astype(jnp.bfloat16)


def place():
    me = lax.axis_index("energy")
    return lax.div(me, 16), lax.rem(lax.div(me, 4), 4), lax.rem(me, 4)


def chip(z, y, x):
    return z * 16 + y * 4 + x


def greet(barrier, ready):
    core = lax.axis_index("mom")
    z, y, x = place()

    def plane(sem):
        @pl.loop(1, 16)
        def _(t):
            c = chip(z, lax.rem(y + lax.div(t, 4), 4), lax.rem(x + lax.rem(t, 4), 4))
            pl.semaphore_signal(sem, inc=1, device_id=(c, core), device_id_type=MESH)

    plane(barrier)
    pl.semaphore_signal(barrier, inc=1, device_id=(chip(z, y, x), 1 - core), device_id_type=MESH)

    @pl.loop(1, 8)
    def _(t):
        c = chip(lax.rem(z + t, 8), y, x)
        for m in range(2):
            pl.semaphore_signal(barrier, inc=1, device_id=(c, m), device_id_type=MESH)

    pl.semaphore_wait(barrier, 30)
    plane(ready)


STEPS = (0, 4, 3, 5, 2, 6, 1, 7)


def line(act):
    core = lax.axis_index("mom")
    z, y, x = place()
    act(chip(z, y, x), 1 - core)
    for dz in STEPS[1:]:
        c = chip(lax.rem(z + dz, 8), y, x)
        act(c, core)
        act(c, 1 - core)


def others(act):
    z, y, x = place()

    @pl.loop(0, 16)
    def _(group):
        for i, dz in enumerate(STEPS):
            own = (-(i // 2)) % 4 * 4 + (-i) % 4

            @pl.when(group != own)
            def _():
                row = lax.rem(y + group + i, 4)
                col = lax.rem(x + lax.div(group, 4) + i // 2, 4)
                act(chip(lax.rem(z + dz, 8), row, col))


def both_cores(remote, core, c):
    remote(c, core)
    remote(c, 1 - core)


def send(remote, local):
    core = lax.axis_index("mom")
    local()
    line(remote)
    others(functools.partial(both_cores, remote, core))


def send_to(q, remote, local):
    core = lax.axis_index("mom")
    z, y, x = place()

    @pl.when(core == q)
    def _():
        local()

    @pl.when(core != q)
    def _():
        remote(chip(z, y, x), q)

    for dz in STEPS[1:]:
        remote(chip(lax.rem(z + dz, 8), y, x), q)
    others(lambda c: remote(c, q))


def kernel(
    shift,
    tile_block,
    lesser,
    greater,
    coulomb,
    tf_hbm,
    ti_hbm,
    pol_out,
    scr_out,
    src,
    got,
    spec,
    mix,
    polar,
    near,
    near_got,
    tf,
    ti,
    weights,
    swap,
    ready,
    load_sem,
    in_send,
    in_recv,
    pol_send,
    pol_recv,
    near_send,
    near_recv,
):
    me = lax.axis_index("energy")
    core = lax.axis_index("mom")
    loads = [
        pltpu.make_async_copy(lesser.at[0], src.at[0], load_sem.at[0]),
        pltpu.make_async_copy(greater.at[0], src.at[1], load_sem.at[1]),
        pltpu.make_async_copy(tf_hbm, tf, load_sem.at[2]),
        pltpu.make_async_copy(ti_hbm, ti, load_sem.at[3]),
    ]
    for load in loads:
        load.start()

    barrier = pltpu.get_barrier_semaphore()
    greet(barrier, ready)
    for load in loads[:2]:
        load.wait()

    def copies(source, target, send_sem, recv_sem):
        def remote(c, m):
            pltpu.make_async_remote_copy(
                source(c, m), target, send_sem, recv_sem, device_id=(c, m), device_id_type=MESH
            ).start()

        def local():
            pltpu.make_async_copy(source(me, core), target, recv_sem).start()

        return remote, local

    def copies_in(b):
        def source(c, m):
            column = pl.multiple_of((c * 2 + m) * 2 * PART + b * PART, PART)
            return src.at[:, :, :, pl.ds(column, PART)]

        return copies(source, got.at[b, :, :, core, me], in_send.at[b], in_recv.at[b])

    def copies_pol(b):
        column = pl.multiple_of((me * 2 + core) * 2 * PART + b * PART, PART)
        return copies(
            lambda c, m: polar.at[b, m, :, c],
            pol_out.at[0, :, :, pl.ds(column, PART)],
            pol_send.at[b],
            pol_recv,
        )

    def copies_near():
        place_of = near_got.at[lax.div(me, 32), lax.rem(me, 32), core]
        return copies(lambda c, m: near.at[m, c], place_of, near_send, near_recv)

    def wait_all(ref, sem):
        pltpu.make_async_copy(ref, ref, sem).wait()

    sent = pl.ds(0, (2 * CHIPS - 1) * PART)
    for b in range(2):
        remote, local = copies_in(b)
        line(remote)
        local()
    pl.semaphore_wait(ready, 15)
    for b in range(2):
        remote, _ = copies_in(b)
        others(functools.partial(both_cores, remote, core))
    prepare(coulomb, weights, swap)
    for load in loads[2:]:
        load.wait()
    for b in range(2):
        wait_all(got.at[b], in_recv.at[b])
        forward(got, b, tf, spec)
        for q in range(2):
            products(q, shift, spec, mix)
            backward(q, b, ti, mix, swap, polar, near)
            if b == 1:
                send_to(q, *copies_near())
                send_to(q, *copies_pol(b))
        if b == 0:
            send(*copies_pol(b))
    wait_all(near_got, near_recv)
    screening(tile_block, weights, near_got, scr_out)
    wait_all(pol_out, pol_recv)
    for b in range(2):
        wait_all(src.at[:, :, :, sent], in_send.at[b])
        wait_all(src.at[0, :, :, sent], pol_send.at[b])
    wait_all(src.at[0, 0, :, sent], near_send)


def shards(lesser, greater, coulomb, tile_block, shift_table):
    tf, ti = tables()
    bf16, f32 = jnp.bfloat16, jnp.float32
    hbm = pl.BlockSpec(memory_space=pl.ANY)
    smem = pl.BlockSpec(memory_space=pltpu.SMEM)
    vmem = pl.BlockSpec(memory_space=pltpu.VMEM)
    operands = (shift_table, tile_block, lesser, greater, coulomb, jnp.asarray(tf), jnp.asarray(ti))
    polarization, screened = pl.pallas_call(
        kernel,
        out_shape=(
            jax.ShapeDtypeStruct((1, 2, E // CHIPS, NNZ), bf16),
            jax.ShapeDtypeStruct((2, 4, L, PART), f32),
        ),
        in_specs=[smem, smem, hbm, hbm, vmem, hbm, hbm],
        out_specs=(hbm, vmem),
        scratch_shapes=[
            pltpu.VMEM((2, 2, E // CHIPS, NNZ), bf16),
            pltpu.VMEM((2, 2, 2, 2, CHIPS, E // CHIPS, PART), bf16),
            pltpu.VMEM((2, 2, BLOCKS, 2, FREQ, PART), f32),
            pltpu.VMEM((2, 2, BLOCKS, 2, FREQ, PART), bf16),
            pltpu.VMEM((2, 2, 2, CHIPS, E // CHIPS, PART), bf16),
            pltpu.VMEM((2, L, 2, 2, PART), bf16),
            pltpu.VMEM((4, 32, 2, 2, 2, PART), bf16),
            pltpu.VMEM((2, 2 * FREQ, 2 * L), bf16),
            pltpu.VMEM((2, 2 * L, 2 * FREQ), bf16),
            pltpu.VMEM((2, 2 * L, 4 * L), bf16),
            pltpu.VMEM((2 * L, 2 * L), bf16),
            pltpu.SemaphoreType.REGULAR,
            pltpu.SemaphoreType.DMA((4,)),
            pltpu.SemaphoreType.DMA((2,)),
            pltpu.SemaphoreType.DMA((2,)),
            pltpu.SemaphoreType.DMA((2,)),
            pltpu.SemaphoreType.DMA,
            pltpu.SemaphoreType.DMA,
            pltpu.SemaphoreType.DMA,
        ],
        compiler_params=pltpu.CompilerParams(
            collective_id=0, has_side_effects=True, vmem_limit_bytes=48 << 20
        ),
        name="polarization",
    )(*(pltpu.with_memory_space_constraint(operand, pltpu.HBM) for operand in operands))
    return (polarization, screened.reshape(1, 2, 1, NNZ))


def solution(mesh):
    return jax.shard_map(
        shards,
        mesh=mesh,
        in_specs=(
            P("mom", None, "energy", None),
            P("mom", None, "energy", None),
            P("mom", None, None, None),
            P(),
            P(),
        ),
        out_specs=(P("mom", None, "energy", None), P("mom", None, "energy", None)),
        check_vma=False,
    )
```

```python
import functools
import math

import jax
import jax.numpy as jnp
import numpy as np
from jax import lax
from jax.experimental import pallas as pl
from jax.experimental.pallas import tpu as pltpu
from jax.sharding import PartitionSpec as P

E = 512
L = 128
FREQ = 2 * L
BLOCKS = E // L
CHIPS = 128
NNZ = 65536
PART = 128
MESH = pl.DeviceIdType.MESH


def split(table):
    high = table.astype(jnp.bfloat16)
    low = (table - high.astype(np.float64)).astype(jnp.bfloat16)
    return np.stack([high, low])


def tables():
    freq = np.concatenate([np.arange(0, FREQ, 2), np.arange(1, FREQ, 2)])
    angle = 2.0 * np.pi / FREQ * ((freq[:, None] * np.arange(L)[None, :]) % FREQ)
    cos, sin = np.cos(angle), np.sin(angle)
    forward = np.block([[cos, sin], [-sin, cos]])
    scale = 1.0 / (math.sqrt(2 * E) * FREQ)
    inverse = np.block([[-sin.T, -cos.T], [cos.T, -sin.T]]) * scale
    return split(forward), split(inverse)


def dot(a, b):
    return jnp.dot(a, b, preferred_element_type=jnp.float32)


def forward(got, b, tf, spec):
    @pl.loop(0, 8)
    def _(step):
        g, k, pair = step // 4, (step // 2) % 2, step % 2
        halves = []
        for h in range(2):
            rows = pl.ds((pair * 2 + h) * 32, 32)
            parts = [got[b, g, s, k, rows].reshape(L, PART) for s in range(2)]
            halves.append(jnp.concatenate(parts, axis=0))
        data = jnp.concatenate(halves, axis=1)
        result = dot(tf[0], data) + dot(tf[1], data)
        for h in range(2):
            for part in range(2):
                spec[g, k, pair * 2 + h, part] = result[
                    part * FREQ : (part + 1) * FREQ, h * PART : (h + 1) * PART
                ]


def products(q, shift, spec, mix):
    for odd in range(2):

        @pl.loop(0, L // 16)
        def _(tile):
            rows = pl.ds(pl.multiple_of(odd * L + tile * 16, 16), 16)
            total = [[None, None] for _ in range(BLOCKS)]

            def add(d, part, value):
                old = total[d][part]
                total[d][part] = value if old is None else old + value

            for k in range(2):
                other = shift[q, k]
                left = [[spec[0, k, a, part, rows] for part in range(2)] for a in range(BLOCKS)]
                for c in range(BLOCKS):
                    right_re = spec[1, other, c, 0, rows]
                    right_im = spec[1, other, c, 1, rows]
                    for d in range(BLOCKS - c):
                        re, im = left[c + d]
                        add(d, 0, re * right_re + im * right_im)
                        add(d, 1, im * right_re - re * right_im)
            for d in range(BLOCKS):
                for part in range(2):
                    value = total[d][part]
                    if d + 1 < BLOCKS:
                        nxt = total[d + 1][part]
                        value = value - nxt if odd else value + nxt
                    high = value.astype(jnp.bfloat16)
                    low = (value - high.astype(jnp.float32)).astype(jnp.bfloat16)
                    mix[0, q, d, part, rows] = high
                    mix[1, q, d, part, rows] = low


def backward(q, b, ti, mix, swap, polar, near):
    for pair in range(2):
        datas = []
        for level in range(2):
            halves = [mix[level, q, pair * 2 + h].reshape(2 * FREQ, PART) for h in range(2)]
            datas.append(jnp.concatenate(halves, axis=1))
        result = dot(ti[0], datas[0]) + dot(ti[0], datas[1]) + dot(ti[1], datas[0])
        result = result.astype(jnp.bfloat16)
        for h in range(2):
            for s in range(2):
                value = result[s * L : (s + 1) * L, h * PART : (h + 1) * PART]
                polar[b, q, s, pl.ds((pair * 2 + h) * 32, 32)] = value.reshape(32, 4, PART)
        if pair == 0:
            value = dot(swap[...], result[:, :PART]).astype(jnp.bfloat16)
            near[q, :, b] = value.reshape(L, 2, PART)


def screening(tile_block, weights, got, out):
    place = []
    for label in range(4):
        where = jnp.int32(0)
        for t in range(1, 4):
            where = jnp.where(tile_block[t] == label, t, where)
        place.append(where)
    sides = []
    for l in range(2):
        tiles = [got[place[2 * l + c]].reshape(2 * L, PART) for c in range(2)]
        sides.append(jnp.concatenate(tiles, axis=1))
    data = jnp.concatenate(sides, axis=0)
    for r in range(2):
        result = dot(weights[r], data)
        for c in range(2):
            for s in range(2):
                out[s, 2 * r + c] = result[s * L : (s + 1) * L, c * PART : (c + 1) * PART]


def prepare(coulomb, weights, swap):
    row = lax.broadcasted_iota(jnp.int32, (2 * L, 2 * L), 0)
    col = lax.broadcasted_iota(jnp.int32, (2 * L, 2 * L), 1)
    swap[...] = jnp.where(col == (row % 2) * L + row // 2, 1.0, 0.0).astype(jnp.bfloat16)
    wide_row = lax.broadcasted_iota(jnp.int32, (L, 2 * L), 0)
    wide_col = lax.broadcasted_iota(jnp.int32, (L, 2 * L), 1)
    for s in range(2):
        spread = jnp.where(wide_col == 2 * wide_row + s, 1.0, 0.0).astype(jnp.bfloat16)
        for r in range(2):
            for l in range(2):
                weights[r, s * L : (s + 1) * L, l * 2 * L : (l + 1) * 2 * L] = dot(
                    coulomb[0, 2 * r + l], spread
                ).astype(jnp.bfloat16)


def place():
    me = lax.axis_index("energy")
    return lax.div(me, 16), lax.rem(lax.div(me, 4), 4), lax.rem(me, 4)


def chip(z, y, x):
    return z * 16 + y * 4 + x


def greet(barrier, ready, loads):
    core = lax.axis_index("mom")
    z, y, x = place()

    def plane(sem):
        @pl.loop(1, 16)
        def _(t):
            c = chip(z, lax.rem(y + lax.div(t, 4), 4), lax.rem(x + lax.rem(t, 4), 4))
            pl.semaphore_signal(sem, inc=1, device_id=(c, core), device_id_type=MESH)

    plane(barrier)
    pl.semaphore_signal(barrier, inc=1, device_id=(chip(z, y, x), 1 - core), device_id_type=MESH)

    @pl.loop(1, 8)
    def _(t):
        c = chip(lax.rem(z + t, 8), y, x)
        for m in range(2):
            pl.semaphore_signal(barrier, inc=1, device_id=(c, m), device_id_type=MESH)

    for load in loads:
        load.start()
    pl.semaphore_wait(barrier, 30)
    plane(ready)
    for load in loads:
        load.wait()


STEPS = (0, 4, 3, 5, 2, 6, 1, 7)


def line(act):
    core = lax.axis_index("mom")
    z, y, x = place()
    act(chip(z, y, x), 1 - core)
    for dz in STEPS[1:]:
        c = chip(lax.rem(z + dz, 8), y, x)
        act(c, core)
        act(c, 1 - core)


def others(act):
    z, y, x = place()

    @pl.loop(0, 16)
    def _(group):
        for i, dz in enumerate(STEPS):
            own = (-(i // 2)) % 4 * 4 + (-i) % 4

            @pl.when(group != own)
            def _():
                row = lax.rem(y + group + i, 4)
                col = lax.rem(x + lax.div(group, 4) + i // 2, 4)
                act(chip(lax.rem(z + dz, 8), row, col))


def both_cores(remote, core, c):
    remote(c, core)
    remote(c, 1 - core)


def send(remote, local):
    core = lax.axis_index("mom")
    local()
    line(remote)
    others(functools.partial(both_cores, remote, core))


def send_to(q, remote, local):
    core = lax.axis_index("mom")
    z, y, x = place()

    @pl.when(core == q)
    def _():
        local()

    @pl.when(core != q)
    def _():
        remote(chip(z, y, x), q)

    for dz in STEPS[1:]:
        remote(chip(lax.rem(z + dz, 8), y, x), q)
    others(lambda c: remote(c, q))


def kernel(
    shift_hbm,
    tile_hbm,
    lesser,
    greater,
    coulomb_hbm,
    tf_hbm,
    ti_hbm,
    pol_out,
    scr_out,
    shift,
    tile_block,
    coulomb,
    screened,
    src,
    got,
    spec,
    mix,
    polar,
    near,
    near_got,
    tf,
    ti,
    weights,
    swap,
    ready,
    load_sem,
    in_send,
    in_recv,
    pol_send,
    pol_recv,
    near_send,
    near_recv,
):
    me = lax.axis_index("energy")
    core = lax.axis_index("mom")
    loads = [
        pltpu.make_async_copy(lesser.at[0], src.at[0], load_sem.at[0]),
        pltpu.make_async_copy(greater.at[0], src.at[1], load_sem.at[1]),
        pltpu.make_async_copy(tf_hbm, tf, load_sem.at[2]),
        pltpu.make_async_copy(ti_hbm, ti, load_sem.at[3]),
        pltpu.make_async_copy(shift_hbm, shift, load_sem.at[4]),
        pltpu.make_async_copy(tile_hbm, tile_block, load_sem.at[5]),
        pltpu.make_async_copy(coulomb_hbm, coulomb, load_sem.at[6]),
    ]
    greet(pltpu.get_barrier_semaphore(), ready, loads[:2])
    for load in loads[2:]:
        load.start()

    def copies(source, target, send_sem, recv_sem):
        def remote(c, m):
            pltpu.make_async_remote_copy(
                source(c, m), target, send_sem, recv_sem, device_id=(c, m), device_id_type=MESH
            ).start()

        def local():
            pltpu.make_async_copy(source(me, core), target, recv_sem).start()

        return remote, local

    def copies_in(b):
        def source(c, m):
            column = pl.multiple_of((c * 2 + m) * 2 * PART + b * PART, PART)
            return src.at[:, :, :, pl.ds(column, PART)]

        return copies(source, got.at[b, :, :, core, me], in_send.at[b], in_recv.at[b])

    def copies_pol(b):
        column = pl.multiple_of((me * 2 + core) * 2 * PART + b * PART, PART)
        return copies(
            lambda c, m: polar.at[b, m, :, c],
            pol_out.at[0, :, :, pl.ds(column, PART)],
            pol_send.at[b],
            pol_recv,
        )

    def copies_near():
        place_of = near_got.at[lax.div(me, 32), lax.rem(me, 32), core]
        return copies(lambda c, m: near.at[m, c], place_of, near_send, near_recv)

    def wait_all(ref, sem):
        pltpu.make_async_copy(ref, ref, sem).wait()

    sent = pl.ds(0, (2 * CHIPS - 1) * PART)
    for b in range(2):
        remote, local = copies_in(b)
        line(remote)
        local()
    pl.semaphore_wait(ready, 15)
    for b in range(2):
        remote, _ = copies_in(b)
        others(functools.partial(both_cores, remote, core))
    for load in loads[2:]:
        load.wait()
    prepare(coulomb, weights, swap)
    for b in range(2):
        wait_all(got.at[b], in_recv.at[b])
        forward(got, b, tf, spec)
        for q in range(2):
            products(q, shift, spec, mix)
            backward(q, b, ti, mix, swap, polar, near)
            if b == 1:
                send_to(q, *copies_near())
                send_to(q, *copies_pol(b))
        if b == 0:
            send(*copies_pol(b))
    wait_all(near_got, near_recv)
    screening(tile_block, weights, near_got, screened)
    store = pltpu.make_async_copy(screened, scr_out, load_sem.at[7])
    store.start()
    wait_all(pol_out, pol_recv)
    store.wait()
    for b in range(2):
        wait_all(src.at[:, :, :, sent], in_send.at[b])
        wait_all(src.at[0, :, :, sent], pol_send.at[b])
    wait_all(src.at[0, 0, :, sent], near_send)


def shards(lesser, greater, coulomb, tile_block, shift_table):
    tf, ti = tables()
    bf16, f32 = jnp.bfloat16, jnp.float32
    hbm = pl.BlockSpec(memory_space=pl.ANY)
    operands = (shift_table, tile_block, lesser, greater, coulomb, jnp.asarray(tf), jnp.asarray(ti))
    polarization, screened = pl.pallas_call(
        kernel,
        out_shape=(
            jax.ShapeDtypeStruct((1, 2, E // CHIPS, NNZ), bf16),
            jax.ShapeDtypeStruct((2, 4, L, PART), f32),
        ),
        in_specs=[hbm] * 7,
        out_specs=(hbm, hbm),
        scratch_shapes=[
            pltpu.SMEM((2, 2), jnp.int32),
            pltpu.SMEM((4,), jnp.int32),
            pltpu.VMEM((1, 4, L, PART), bf16),
            pltpu.VMEM((2, 4, L, PART), f32),
            pltpu.VMEM((2, 2, E // CHIPS, NNZ), bf16),
            pltpu.VMEM((2, 2, 2, 2, CHIPS, E // CHIPS, PART), bf16),
            pltpu.VMEM((2, 2, BLOCKS, 2, FREQ, PART), f32),
            pltpu.VMEM((2, 2, BLOCKS, 2, FREQ, PART), bf16),
            pltpu.VMEM((2, 2, 2, CHIPS, E // CHIPS, PART), bf16),
            pltpu.VMEM((2, L, 2, 2, PART), bf16),
            pltpu.VMEM((4, 32, 2, 2, 2, PART), bf16),
            pltpu.VMEM((2, 2 * FREQ, 2 * L), bf16),
            pltpu.VMEM((2, 2 * L, 2 * FREQ), bf16),
            pltpu.VMEM((2, 2 * L, 4 * L), bf16),
            pltpu.VMEM((2 * L, 2 * L), bf16),
            pltpu.SemaphoreType.REGULAR,
            pltpu.SemaphoreType.DMA((8,)),
            pltpu.SemaphoreType.DMA((2,)),
            pltpu.SemaphoreType.DMA((2,)),
            pltpu.SemaphoreType.DMA((2,)),
            pltpu.SemaphoreType.DMA,
            pltpu.SemaphoreType.DMA,
            pltpu.SemaphoreType.DMA,
        ],
        compiler_params=pltpu.CompilerParams(
            collective_id=0, has_side_effects=True, vmem_limit_bytes=48 << 20
        ),
        name="polarization",
    )(*(pltpu.with_memory_space_constraint(operand, pltpu.HBM) for operand in operands))
    return (polarization, screened.reshape(1, 2, 1, NNZ))


def solution(mesh):
    return jax.shard_map(
        shards,
        mesh=mesh,
        in_specs=(
            P("mom", None, "energy", None),
            P("mom", None, "energy", None),
            P("mom", None, None, None),
            P(),
            P(),
        ),
        out_specs=(P("mom", None, "energy", None), P("mom", None, "energy", None)),
        check_vma=False,
    )
```
